32 devices in a mesh: qx: 8 (over z, y), qy: 4 (over x, core).
Axes of the slice: x: 2, y: 2, z: 4, core: 2. Of those that a mesh axis runs over, the one named last changes fastest.
Arguments:
- vectors: bfloat16 [64, 256, 512], P(None, 'qx', 'qy'), may hold values from -6 to 6
- near_tiles: bfloat16 [16, 32, 3, 256, 256], P('qx', 'qy'), may hold values from -0.21875 to 0.21875
- near_offset: int32 [16, 32, 3], P('qx', 'qy'), may hold values from 0 to 8, as said below
- col_basis: bfloat16 [16, 32, 64, 256], P('qx', 'qy'), may hold values from -0.375 to 0.375
- row_basis: bfloat16 [16, 32, 64, 256], P('qx', 'qy'), may hold values from -0.375 to 0.375
- up_transfer: float32 [16, 32, 64, 64], P('qx', 'qy'), may hold values from -0.375 to 0.375
- down_transfer: float32 [16, 32, 64, 64], P('qx', 'qy'), may hold values from -0.75 to 0.75
- coupling: float32 [32, 128, 64, 64], P(('qx', 'qy')), may hold values from -0.75 to 0.75
- couple_dest: int32 [32, 128], replicated, may hold values from -1 to 31, as said below
- couple_target: int32 [32, 128], replicated, may hold values from 0 to 19, as said below
Outputs:
- product: float32 [64, 256, 512], P(None, 'qx', 'qy')
The draws below stay inside these ranges and needn't reach their ends.
Inputs may be any that keep to these rules, and one draw needn't show every extreme that they name: `couple_dest`: in each row (source device) no destination device appears more than 4 times; in every draw one destination device appears exactly 4 times in every row; -1 marks a padded slot. `couple_target`: slots below 96 name a leaf cluster (0 to 15), the others a parent cluster (16 to 19) of the target device. `near_offset`: the 3 codes of a leaf are distinct; code o reads the leaf at offset (o // 3 - 1, o % 3 - 1).
All inputs are finite; a program needn't handle non-finite values.
Results may differ from the reference program's by a relative error of at most 0.0003.
Values may be sent and summed in bfloat16 or wider, within the bound.
A program may use at most 64 MiB of HBM per device.

```python
import jax
import jax.numpy as jnp
from jax import lax

R = 64
VECS = 64
LS = 16
NEAR = 3
K0 = 6
K1 = 8
CY = 128
LP = 256
LEAVES_DEV = 16
L1_DEV = 4
CLUSTERS = 20
SLOTS = 128
CAP = 4
NX = 256
NY = 512
GX = 16
GY = 32
N_QX = 8
N_QY = 4
DEVICES = 32


def draw_couple_dest(key, part):
    key = jax.random.fold_in(key, 101)
    key_hot, key_order, key_shuffle, key_live = jax.random.split(key, 4)
    total = DEVICES * CAP
    hot_device = jax.random.randint(key_hot, (), 0, DEVICES)
    ident = jnp.arange(total, dtype=jnp.int32)
    owner = ident // CAP
    scores = jax.random.randint(key_order, (DEVICES, total), 0, 1 << 20) * total + ident[None, :]
    scores = jnp.where(owner[None, :] == hot_device, ident[None, :] - total, scores)
    chosen = jnp.argsort(scores, axis=1)[:, :SLOTS].astype(jnp.int32)
    dest = chosen // CAP
    slot_ident = jnp.arange(SLOTS, dtype=jnp.int32)
    shuffle = jnp.argsort(jax.random.randint(key_shuffle, (DEVICES, SLOTS), 0, 1 << 20) * SLOTS + slot_ident[None, :], axis=1).astype(jnp.int32)
    dest = jnp.take_along_axis(dest, shuffle, axis=1)
    live = (jax.random.randint(key_live, (DEVICES, SLOTS), 0, 20) >= 3) | (dest == hot_device)
    return jnp.where(live, dest, -1).astype(jnp.int32)


def draw_couple_target(key, part):
    key = jax.random.fold_in(key, 202)
    drawn = jax.random.randint(key, (DEVICES, SLOTS), 0, 1 << 20)
    column = jnp.arange(SLOTS, dtype=jnp.int32)[None, :]
    leaf_part = column < LEAVES_DEV * K0
    return jnp.where(leaf_part, drawn % LEAVES_DEV, LEAVES_DEV + drawn % L1_DEV).astype(jnp.int32)


def draw_near_offset(key, part):
    key = jax.random.fold_in(key, 303)
    scores = jax.random.randint(key, (GX, GY, 9), 0, 1 << 20) * 9 + jnp.arange(9, dtype=jnp.int32)
    return jnp.argsort(scores, axis=2)[:, :, :NEAR].astype(jnp.int32)


def levels(own_key, extent, cuts, low, largest):
    gain = 1.0
    for position, blocks in cuts:
        draws = jax.random.uniform(jax.random.fold_in(jax.random.fold_in(own_key, 6), position), (blocks,), jnp.float32, low / len(cuts), largest / len(cuts))
        gain = gain * jnp.repeat(jnp.exp(draws), extent[position] // blocks).reshape((-1,) + (1,) * (len(extent) - 1 - position))
    return gain


def bell_draw(own_key, dims, deviation, bound, cuts=(), kind=jnp.bfloat16):
    values = jax.random.normal(own_key, dims, jnp.float32) * deviation
    if len(cuts) > 0:
        values = levels(own_key, dims, cuts, -0.22, 0.18) * values
    return jnp.clip(values, min=-bound, max=bound).astype(kind)


def setup_inputs(seed: int = 0) -> dict:
    key_list = jax.random.split(jax.random.key(seed), 11)
    vectors = bell_draw(key_list[0], (VECS, NX, NY), 1.0, 6.0, ((1, 8), (2, 4)))
    near_tiles = bell_draw(key_list[1], (GX, GY, NEAR, LP, LP), (NEAR * LP) ** -0.5, 0.21875, ((0, 8), (1, 4)))
    near_offset = draw_near_offset(jax.random.fold_in(key_list[10], 71), 0)
    col_basis = bell_draw(key_list[3], (GX, GY, R, LP), LP ** -0.5, 0.375, ((0, 8), (1, 4)))
    row_basis = bell_draw(key_list[4], (GX, GY, R, LP), LP ** -0.5, 0.375, ((0, 8), (1, 4)))
    up_transfer = bell_draw(key_list[5], (GX, GY, R, R), (4 * R) ** -0.5, 0.375, ((0, 8), (1, 4)), jnp.float32)
    down_transfer = bell_draw(key_list[6], (GX, GY, R, R), R ** -0.5, 0.75, ((0, 8), (1, 4)), jnp.float32)
    coupling = bell_draw(key_list[7], (DEVICES, SLOTS, R, R), R ** -0.5, 0.75, ((0, 32),), jnp.float32)
    couple_dest = draw_couple_dest(jax.random.fold_in(key_list[10], 71), 0)
    couple_target = draw_couple_target(jax.random.fold_in(key_list[10], 71), 0)
    return dict(vectors=vectors, near_tiles=near_tiles, near_offset=near_offset, col_basis=col_basis, row_basis=row_basis, up_transfer=up_transfer, down_transfer=down_transfer, coupling=coupling, couple_dest=couple_dest, couple_target=couple_target)


def reference(vectors, near_tiles, near_offset, col_basis, row_basis, up_transfer, down_transfer, coupling, couple_dest, couple_target):
    precise = lax.Precision.HIGHEST
    grid_x = NX // LS
    grid_y = NY // LS
    leaf_y = CY // LS
    devices = N_QX * N_QY
    blocks = vectors.reshape(VECS, grid_x, LS, grid_y, LS).transpose(1, 3, 0, 2, 4).reshape(grid_x, grid_y, VECS, LP)
    leaf_coef = jnp.einsum('ijrp,ijvp->ijrv', col_basis.astype(jnp.float32), blocks.astype(jnp.float32), precision=precise)
    lifted = jnp.einsum('ijrs,ijsv->ijrv', up_transfer, leaf_coef, precision=precise)
    upper_coef = lifted.reshape(grid_x // 2, 2, grid_y // 2, 2, R, VECS).sum(axis=(1, 3))
    leaf_dev = leaf_coef.reshape(N_QX, 2, N_QY, leaf_y, R, VECS).transpose(0, 2, 1, 3, 4, 5).reshape(devices, LEAVES_DEV, R, VECS)
    upper_dev = upper_coef.reshape(N_QX, N_QY, L1_DEV, R, VECS).reshape(devices, L1_DEV, R, VECS)

    def send_step(totals, device_item):
        leaf_part, upper_part, couple_block, dest_row, target_row = device_item
        source_coef = jnp.concatenate([jnp.repeat(leaf_part, K0, axis=0), jnp.repeat(upper_part, K1, axis=0)], axis=0)
        contrib = jnp.einsum('srt,stv->srv', couple_block, source_coef, precision=precise).reshape(SLOTS, R * VECS)
        segment_ids = jnp.where(dest_row >= 0, dest_row * CLUSTERS + target_row, devices * CLUSTERS).astype(jnp.int32)
        return totals.at[segment_ids].add(contrib), None

    totals = jnp.zeros((devices * CLUSTERS + 1, R * VECS), jnp.float32)
    totals, _ = lax.scan(send_step, totals, (leaf_dev, upper_dev, coupling, couple_dest, couple_target))
    gathered = totals[:devices * CLUSTERS].reshape(devices, CLUSTERS, R, VECS)
    down_leaf = gathered[:, :LEAVES_DEV].reshape(N_QX, N_QY, 2, leaf_y, R, VECS).transpose(0, 2, 1, 3, 4, 5).reshape(grid_x, grid_y, R, VECS)
    down_upper = gathered[:, LEAVES_DEV:].reshape(N_QX, N_QY * L1_DEV, R, VECS)
    expanded = jnp.repeat(jnp.repeat(down_upper, 2, axis=0), 2, axis=1)
    down_leaf = down_leaf + jnp.einsum('ijrs,ijsv->ijrv', down_transfer, expanded, precision=precise)
    far_out = jnp.einsum('ijrp,ijrv->ijvp', row_basis.astype(jnp.float32), down_leaf, precision=precise)

    padded = jnp.pad(vectors, ((0, 0), (LS, LS), (LS, LS)))
    padded_blocks = padded.reshape(VECS, grid_x + 2, LS, grid_y + 2, LS).transpose(1, 3, 0, 2, 4).reshape((grid_x + 2) * (grid_y + 2), VECS, LP)
    along_x = jnp.arange(grid_x, dtype=jnp.int32)[:, None, None]
    along_y = jnp.arange(grid_y, dtype=jnp.int32)[None, :, None]
    tile_index = ((along_x + near_offset // 3) * (grid_y + 2) + along_y + near_offset % 3).astype(jnp.int32)

    def near_row(leaf_row):
        tiles = near_tiles[leaf_row].astype(jnp.float32)
        picked = padded_blocks[tile_index[leaf_row]].astype(jnp.float32)
        return jnp.einsum('jkps,jkvs->jvp', tiles, picked, precision=precise)

    near_out = lax.map(near_row, jnp.arange(grid_x, dtype=jnp.int32))
    total_out = near_out + far_out
    return total_out.reshape(grid_x, grid_y, VECS, LS, LS).transpose(2, 0, 3, 1, 4).reshape(VECS, NX, NY)
```

```python
import jax
import jax.numpy as jnp
from jax import lax
from jax.experimental import pallas as pl
from jax.experimental.pallas import tpu as pltpu
from jax.sharding import PartitionSpec as P

LS = 16
K0 = 6
K1 = 8


def extended(array, sides, width):
    for axis, dim in sides:
        peers, length = (lax.axis_size(axis), array.shape[dim])
        up = [(i, (i + 1) % peers) for i in range(peers - 1)]
        down = [(j, i) for i, j in up]
        last = lax.slice_in_dim(array, length - width, length, axis=dim)
        initial = lax.slice_in_dim(array, 0, width, axis=dim)
        before = lax.ppermute(last, axis, up)
        after = lax.ppermute(initial, axis, down)
        array = jnp.concatenate([before, array, after], axis=dim)
    return array


VM = pl.BlockSpec(memory_space=pltpu.VMEM)
SM = pl.BlockSpec(memory_space=pltpu.SMEM)
TOP = 14


def halves(value):
    high = value.astype(jnp.bfloat16)
    return high, (value - high.astype(jnp.float32)).astype(jnp.bfloat16)


def product_of(left, right):
    lh, ll = halves(left)
    rh, rl = halves(right)
    return jnp.dot(
        jnp.concatenate([lh, ll, lh, ll], axis=1),
        jnp.concatenate([rh, rh, rl, rl], axis=0),
        preferred_element_type=jnp.float32,
    )


def contrib_kernel(leaf_count, upper_count, pos_ref, coup_ref, leaf_ref, upper_ref, out_ref, max_ref):
    rank = coup_ref.shape[1]
    half = rank // 2
    out_ref[...] = jnp.zeros_like(out_ref)
    max_ref[...] = jnp.zeros_like(max_ref)

    def group(first, count, coef):
        mats = coup_ref[pl.ds(first, count)].reshape(count * rank, rank)
        res = product_of(mats, coef)
        for q in range(count):
            row = pos_ref[first + q]
            one = res[q * rank : (q + 1) * rank]
            folded = jnp.concatenate([one[:half], one[half:]], axis=1)
            out_ref[row] = folded
            max_ref[row] = jnp.max(jnp.abs(folded), axis=0, keepdims=True)

    def leaf_step(m, carry):
        group(m * K0, K0, leaf_ref[m])
        return carry

    def upper_step(m, carry):
        group(leaf_count * K0 + m * K1, K1, upper_ref[m])
        return carry

    lax.fori_loop(0, leaf_count, leaf_step, 0)
    lax.fori_loop(0, upper_count, upper_step, 0)


def near_kernel(leaf_y, off_ref, tiles_ref, grid_ref, out_ref):
    m = pl.program_id(0)
    i = m // leaf_y
    j = lax.rem(m, leaf_y)
    vecs = grid_ref.shape[2]
    total = None
    for k in range(tiles_ref.shape[1]):
        o = off_ref[m, k]
        x = (i + o // 3) * LS
        y = pl.multiple_of((j + lax.rem(o, 3)) * LS, LS)
        block = grid_ref[pl.ds(x, LS), pl.ds(y, LS), :].reshape(LS * LS, vecs)
        term = jnp.dot(tiles_ref[0, k], block, preferred_element_type=jnp.float32)
        total = term if total is None else total + term
    out_ref[0] = total


def far_kernel(leaf_x, leaf_y, tgt_ref, recv_ref, down_ref, row_ref, near_ref, out_ref, acc, full):
    leaf_count = leaf_x * leaf_y
    half = acc.shape[2] // 2
    acc[...] = jnp.zeros_like(acc)

    def add(r, carry):
        t = tgt_ref[r]
        acc[t] = acc[t] + recv_ref[r]
        return carry

    lax.fori_loop(0, recv_ref.shape[0], add, 0, unroll=4)

    def unfolded(n):
        value = acc[n]
        return jnp.concatenate([value[:, :half], value[:, half:]], axis=0)

    def leaf(m, carry):
        j = lax.rem(m, leaf_y)
        coef = unfolded(m) + product_of(down_ref[m], unfolded(leaf_count + j // 2))
        high, low = halves(coef)
        basis = row_ref[m]
        far = lax.dot_general(
            jnp.concatenate([basis, basis], axis=0),
            jnp.concatenate([high, low], axis=0),
            (((0,), (0,)), ((), ())),
            preferred_element_type=jnp.float32,
        )
        full[m] = near_ref[m] + far
        return carry

    lax.fori_loop(0, leaf_count, leaf, 0)
    for a in range(leaf_x):
        for i in range(LS):
            rows = [full[a * leaf_y + h, i * LS : (i + 1) * LS, :] for h in range(leaf_y)]
            out_ref[:, a * LS + i, :] = jnp.concatenate(rows, axis=0).T


def body(
    vectors,
    near_tiles,
    near_offset,
    col_basis,
    row_basis,
    up_transfer,
    down_transfer,
    coupling,
    couple_dest,
    couple_target,
):
    precise = lax.Precision.HIGHEST
    f32 = jnp.float32
    shape = jax.ShapeDtypeStruct
    width_x = lax.axis_size("qx")
    width_y = lax.axis_size("qy")
    devices = width_x * width_y
    vec_count, rows_x, rows_y = vectors.shape
    leaf_x = rows_x // LS
    leaf_y = rows_y // LS
    leaf_count = leaf_x * leaf_y
    upper_count = leaf_y // 2
    cluster_count = leaf_count + upper_count
    rank_size = coupling.shape[2]
    slot_count = coupling.shape[1]
    capacity = (slot_count + devices - 1) // devices
    near_count = near_tiles.shape[2]
    points = LS * LS
    fold = (rank_size // 2, 2 * vec_count)
    my_index = lax.axis_index("qx") * width_y + lax.axis_index("qy")

    padded = extended(vectors, (("qx", 1), ("qy", 2)), LS)

    blocks = (
        vectors.reshape(vec_count, leaf_x, LS, leaf_y, LS)
        .transpose(1, 3, 0, 2, 4)
        .reshape(leaf_x, leaf_y, vec_count, points)
    )
    leaf_coef = jnp.einsum("ijrp,ijvp->ijrv", col_basis, blocks, preferred_element_type=f32)
    lifted = jnp.einsum("ijrs,ijsv->ijrv", up_transfer, leaf_coef, precision=precise)
    upper_coef = lifted.reshape(leaf_x, upper_count, 2, rank_size, vec_count).sum(axis=(0, 2))

    own_dest = lax.dynamic_index_in_dim(couple_dest, my_index, 0, keepdims=False)
    slot_ident = jnp.arange(slot_count, dtype=jnp.int32)
    same_dest = own_dest[:, None] == own_dest[None, :]
    earlier = slot_ident[:, None] > slot_ident[None, :]
    order_in = jnp.sum((same_dest & earlier).astype(jnp.int32), axis=1)
    spare_row = devices * capacity
    position = jnp.where(own_dest >= 0, own_dest * capacity + order_in, spare_row)
    placed, peaks = pl.pallas_call(
        lambda *refs: contrib_kernel(leaf_count, upper_count, *refs),
        out_shape=(shape((spare_row + 1,) + fold, f32), shape((spare_row + 1, 1, fold[1]), f32)),
        in_specs=[SM, VM, VM, VM],
        out_specs=(VM, VM),
        name="contrib",
    )(position, coupling[0], leaf_coef.reshape(leaf_count, rank_size, vec_count), upper_coef)

    peak = jnp.max(peaks[:spare_row], axis=(1, 2))
    power = jnp.ceil(jnp.log2(jnp.maximum(peak, 1e-30)))
    scaled = placed[:spare_row] * jnp.exp2(TOP - power)[:, None, None]
    notes = jnp.broadcast_to(power.reshape(devices, capacity, 1), (devices, capacity, fold[1]))
    outgoing = jnp.concatenate(
        [
            scaled.reshape(devices, capacity * fold[0], fold[1]).astype(jnp.float16),
            notes.astype(jnp.float16),
        ],
        axis=1,
    )
    outgoing, padded = lax.optimization_barrier((outgoing, padded))
    arrived = lax.all_to_all(outgoing, ("qx", "qy"), split_axis=0, concat_axis=0, tiled=True)

    grid = padded.transpose(1, 2, 0)
    near = pl.pallas_call(
        lambda *refs: near_kernel(leaf_y, *refs),
        grid=(leaf_count,),
        out_shape=shape((leaf_count, points, vec_count), f32),
        in_specs=[
            SM,
            pl.BlockSpec((1, near_count, points, points), lambda m: (m, 0, 0, 0)),
            VM,
        ],
        out_specs=pl.BlockSpec((1, points, vec_count), lambda m: (m, 0, 0)),
        cost_estimate=pl.CostEstimate(
            flops=2 * leaf_count * near_count * points * points * vec_count,
            bytes_accessed=leaf_count * near_count * points * points * 2,
            transcendentals=0,
        ),
        name="near",
    )(
        near_offset.reshape(leaf_count, near_count),
        near_tiles.reshape(leaf_count, near_count, points, points),
        grid,
    )

    matches = couple_dest == my_index
    counts = matches.astype(jnp.int32)
    order = jnp.cumsum(counts, axis=-1) - counts
    landing = matches[:, None, :] & (order[:, None, :] == jnp.arange(capacity, dtype=jnp.int32)[None, :, None])
    target = cluster_count + jnp.sum(
        jnp.where(landing, couple_target[:, None, :] - cluster_count, 0), axis=-1
    )

    rows = capacity * fold[0]
    exponent = arrived[:, rows:, :1].astype(f32).reshape(spare_row, 1, 1)
    recv = arrived[:, :rows].astype(f32).reshape((spare_row,) + fold) * jnp.exp2(exponent - TOP)
    return pl.pallas_call(
        lambda *refs: far_kernel(leaf_x, leaf_y, *refs),
        out_shape=shape((vec_count, rows_x, rows_y), f32),
        in_specs=[SM, VM, VM, VM, VM],
        out_specs=VM,
        scratch_shapes=[
            pltpu.VMEM((cluster_count + 1,) + fold, f32),
            pltpu.VMEM((leaf_count, points, vec_count), f32),
        ],
        name="far",
    )(
        target.reshape(spare_row),
        recv,
        down_transfer.reshape(leaf_count, rank_size, rank_size),
        row_basis.reshape(leaf_count, rank_size, points),
        near,
    )


def solution(mesh):
    return jax.shard_map(
        body,
        mesh=mesh,
        in_specs=(
            P(None, "qx", "qy"),
            P("qx", "qy", None, None, None),
            P("qx", "qy", None),
            P("qx", "qy", None, None),
            P("qx", "qy", None, None),
            P("qx", "qy", None, None),
            P("qx", "qy", None, None),
            P(("qx", "qy"), None, None, None),
            P(),
            P(),
        ),
        out_specs=P(None, "qx", "qy"),
        check_vma=False,
    )
```

```python
import jax
import jax.numpy as jnp
from jax import lax
from jax.experimental import pallas as pl
from jax.experimental.pallas import tpu as pltpu
from jax.sharding import PartitionSpec as P

LS = 16
K0 = 6
K1 = 8


def edges(array, axis, dim, width):
    peers, length = (lax.axis_size(axis), array.shape[dim])
    up = [(i, (i + 1) % peers) for i in range(peers - 1)]
    down = [(j, i) for i, j in up]
    last = lax.slice_in_dim(array, length - width, length, axis=dim)
    initial = lax.slice_in_dim(array, 0, width, axis=dim)
    return [lax.ppermute(last, axis, up), array, lax.ppermute(initial, axis, down)]


VM = pl.BlockSpec(memory_space=pltpu.VMEM)
SM = pl.BlockSpec(memory_space=pltpu.SMEM)
TOP = 14


def halves(value):
    high = value.astype(jnp.bfloat16)
    return high, (value - high.astype(jnp.float32)).astype(jnp.bfloat16)


def product_of(left, right):
    lh, ll = halves(left)
    rh, rl = halves(right)
    return jnp.dot(
        jnp.concatenate([lh, ll, lh, ll], axis=1),
        jnp.concatenate([rh, rh, rl, rl], axis=0),
        preferred_element_type=jnp.float32,
    )


def contrib_kernel(leaf_count, upper_count, pos_ref, coup_ref, leaf_ref, upper_ref, out_ref, max_ref):
    rank = coup_ref.shape[1]
    half = rank // 2
    out_ref[...] = jnp.zeros_like(out_ref)
    max_ref[...] = jnp.zeros_like(max_ref)

    def group(first, count, coef):
        mats = coup_ref[pl.ds(first, count)].reshape(count * rank, rank)
        res = product_of(mats, coef)
        for q in range(count):
            row = pos_ref[first + q]
            one = res[q * rank : (q + 1) * rank]
            folded = jnp.concatenate([one[:half], one[half:]], axis=1)
            out_ref[row] = folded
            max_ref[pl.ds(row, 1), :] = jnp.max(jnp.abs(folded), axis=0, keepdims=True)

    def leaf_step(m, carry):
        group(m * K0, K0, leaf_ref[m])
        return carry

    def upper_step(m, carry):
        group(leaf_count * K0 + m * K1, K1, upper_ref[m])
        return carry

    lax.fori_loop(0, leaf_count, leaf_step, 0, unroll=4)
    lax.fori_loop(0, upper_count, upper_step, 0, unroll=2)


def near_kernel(leaf_y, off_ref, tiles_ref, grid_ref, out_ref):
    m = pl.program_id(0)
    i = m // leaf_y
    j = lax.rem(m, leaf_y)
    vecs = grid_ref.shape[2]
    total = None
    for k in range(tiles_ref.shape[1]):
        o = off_ref[m, k]
        x = (i + o // 3) * LS
        y = pl.multiple_of((j + lax.rem(o, 3)) * LS, LS)
        block = grid_ref[pl.ds(x, LS), pl.ds(y, LS), :].reshape(LS * LS, vecs)
        term = jnp.dot(tiles_ref[0, k], block, preferred_element_type=jnp.float32)
        total = term if total is None else total + term
    out_ref[0] = total


def far_kernel(leaf_x, leaf_y, tgt_ref, recv_ref, down_ref, row_ref, near_ref, out_ref, acc, full):
    leaf_count = leaf_x * leaf_y
    half = acc.shape[2] // 2
    acc[...] = jnp.zeros_like(acc)

    def add(r, carry):
        t = tgt_ref[r]
        acc[t] = acc[t] + recv_ref[r]
        return carry

    lax.fori_loop(0, recv_ref.shape[0], add, 0, unroll=4)

    def unfolded(n):
        value = acc[n]
        return jnp.concatenate([value[:, :half], value[:, half:]], axis=0)

    def leaf(m, carry):
        j = lax.rem(m, leaf_y)
        coef = unfolded(m) + product_of(down_ref[m], unfolded(leaf_count + j // 2))
        high, low = halves(coef)
        basis = row_ref[m]
        far = lax.dot_general(
            jnp.concatenate([basis, basis], axis=0),
            jnp.concatenate([high, low], axis=0),
            (((0,), (0,)), ((), ())),
            preferred_element_type=jnp.float32,
        )
        full[m] = near_ref[m] + far
        return carry

    lax.fori_loop(0, leaf_count, leaf, 0, unroll=4)
    for a in range(leaf_x):
        for i in range(LS):
            rows = [full[a * leaf_y + h, i * LS : (i + 1) * LS, :] for h in range(leaf_y)]
            out_ref[:, a * LS + i, :] = jnp.concatenate(rows, axis=0).T


def body(
    vectors,
    near_tiles,
    near_offset,
    col_basis,
    row_basis,
    up_transfer,
    down_transfer,
    coupling,
    couple_dest,
    couple_target,
):
    precise = lax.Precision.HIGHEST
    f32 = jnp.float32
    shape = jax.ShapeDtypeStruct
    width_x = lax.axis_size("qx")
    width_y = lax.axis_size("qy")
    devices = width_x * width_y
    vec_count, rows_x, rows_y = vectors.shape
    leaf_x = rows_x // LS
    leaf_y = rows_y // LS
    leaf_count = leaf_x * leaf_y
    upper_count = leaf_y // 2
    cluster_count = leaf_count + upper_count
    rank_size = coupling.shape[2]
    slot_count = coupling.shape[1]
    capacity = (slot_count + devices - 1) // devices
    near_count = near_tiles.shape[2]
    points = LS * LS
    fold = (rank_size // 2, 2 * vec_count)
    my_index = lax.axis_index("qx") * width_y + lax.axis_index("qy")

    tall = jnp.concatenate(edges(vectors, "qx", 1, LS), axis=1)
    pieces = edges(tall, "qy", 2, LS)

    blocks = (
        vectors.reshape(vec_count, leaf_x, LS, leaf_y, LS)
        .transpose(1, 3, 0, 2, 4)
        .reshape(leaf_x, leaf_y, vec_count, points)
    )
    leaf_coef = jnp.einsum("ijrp,ijvp->ijrv", col_basis, blocks, preferred_element_type=f32)
    lifted = jnp.einsum("ijrs,ijsv->ijrv", up_transfer, leaf_coef, precision=precise)
    upper_coef = lifted.reshape(leaf_x, upper_count, 2, rank_size, vec_count).sum(axis=(0, 2))

    own_dest = lax.dynamic_index_in_dim(couple_dest, my_index, 0, keepdims=False)
    slot_ident = jnp.arange(slot_count, dtype=jnp.int32)
    same_dest = own_dest[:, None] == own_dest[None, :]
    earlier = slot_ident[:, None] > slot_ident[None, :]
    order_in = jnp.sum((same_dest & earlier).astype(jnp.int32), axis=1)
    spare_row = devices * capacity
    position = jnp.where(own_dest >= 0, own_dest * capacity + order_in, spare_row)
    placed, peaks = pl.pallas_call(
        lambda *refs: contrib_kernel(leaf_count, upper_count, *refs),
        out_shape=(shape((spare_row + 1,) + fold, f32), shape((spare_row + 1, fold[1]), f32)),
        in_specs=[SM, VM, VM, VM],
        out_specs=(VM, VM),
        cost_estimate=pl.CostEstimate(
            flops=8 * slot_count * rank_size * rank_size * vec_count,
            bytes_accessed=16 * slot_count * rank_size * rank_size * 4,
            transcendentals=0,
        ),
        name="contrib",
    )(position, coupling[0], leaf_coef.reshape(leaf_count, rank_size, vec_count), upper_coef)

    peak = jnp.max(peaks[:spare_row], axis=1)
    power = jnp.ceil(jnp.log2(jnp.maximum(peak, 1e-30)))
    scaled = placed[:spare_row] * jnp.exp2(TOP - power)[:, None, None]
    notes = jnp.broadcast_to(power.reshape(devices, capacity, 1), (devices, capacity, fold[1]))
    outgoing = jnp.concatenate(
        [
            scaled.reshape(devices, capacity * fold[0], fold[1]).astype(jnp.float16),
            notes.astype(jnp.float16),
        ],
        axis=1,
    )
    outgoing, pieces = lax.optimization_barrier((outgoing, pieces))
    arrived = lax.all_to_all(outgoing, ("qx", "qy"), split_axis=0, concat_axis=0, tiled=True)

    grid = jnp.concatenate([piece.transpose(1, 2, 0) for piece in pieces], axis=1)
    near = pl.pallas_call(
        lambda *refs: near_kernel(leaf_y, *refs),
        grid=(leaf_count,),
        out_shape=shape((leaf_count, points, vec_count), f32),
        in_specs=[
            SM,
            pl.BlockSpec((1, near_count, points, points), lambda m: (m, 0, 0, 0)),
            VM,
        ],
        out_specs=pl.BlockSpec((1, points, vec_count), lambda m: (m, 0, 0)),
        cost_estimate=pl.CostEstimate(
            flops=2 * leaf_count * near_count * points * points * vec_count,
            bytes_accessed=leaf_count * near_count * points * points * 2,
            transcendentals=0,
        ),
        name="near",
    )(
        near_offset.reshape(leaf_count, near_count),
        near_tiles.reshape(leaf_count, near_count, points, points),
        grid,
    )

    matches = couple_dest == my_index
    counts = matches.astype(jnp.int32)
    order = jnp.cumsum(counts, axis=-1) - counts
    landing = matches[:, None, :] & (order[:, None, :] == jnp.arange(capacity, dtype=jnp.int32)[None, :, None])
    target = cluster_count + jnp.sum(
        jnp.where(landing, couple_target[:, None, :] - cluster_count, 0), axis=-1
    )

    rows = capacity * fold[0]
    exponent = arrived[:, rows:, :1].astype(f32).reshape(spare_row, 1, 1)
    recv = arrived[:, :rows].astype(f32).reshape((spare_row,) + fold) * jnp.exp2(exponent - TOP)
    return pl.pallas_call(
        lambda *refs: far_kernel(leaf_x, leaf_y, *refs),
        out_shape=shape((vec_count, rows_x, rows_y), f32),
        in_specs=[SM, VM, VM, VM, VM],
        out_specs=VM,
        scratch_shapes=[
            pltpu.VMEM((cluster_count + 1,) + fold, f32),
            pltpu.VMEM((leaf_count, points, vec_count), f32),
        ],
        name="far",
    )(
        target.reshape(spare_row),
        recv,
        down_transfer.reshape(leaf_count, rank_size, rank_size),
        row_basis.reshape(leaf_count, rank_size, points),
        near,
    )


def solution(mesh):
    return jax.shard_map(
        body,
        mesh=mesh,
        in_specs=(
            P(None, "qx", "qy"),
            P("qx", "qy", None, None, None),
            P("qx", "qy", None),
            P("qx", "qy", None, None),
            P("qx", "qy", None, None),
            P("qx", "qy", None, None),
            P("qx", "qy", None, None),
            P(("qx", "qy"), None, None, None),
            P(),
            P(),
        ),
        out_specs=P(None, "qx", "qy"),
        check_vma=False,
    )
```

```python
import jax
import jax.numpy as jnp
from jax import lax
from jax.experimental import pallas as pl
from jax.experimental.pallas import tpu as pltpu
from jax.sharding import PartitionSpec as P

LS = 16
K0 = 6
K1 = 8


ANY = pl.BlockSpec(memory_space=pl.ANY)
VM = pl.BlockSpec(memory_space=pltpu.VMEM)
SM = pl.BlockSpec(memory_space=pltpu.SMEM)
TOP = 14


def halves(value):
    high = value.astype(jnp.bfloat16)
    return high, (value - high.astype(jnp.float32)).astype(jnp.bfloat16)


def product_of(left, right):
    lh, ll = halves(left)
    rh, rl = halves(right)
    return jnp.dot(
        jnp.concatenate([lh, ll, lh, ll], axis=1),
        jnp.concatenate([rh, rh, rl, rl], axis=0),
        preferred_element_type=jnp.float32,
    )


def contrib_kernel(leaf_count, upper_count, pos_ref, coup_ref, leaf_ref, upper_ref, out_ref, max_ref):
    rank = coup_ref.shape[1]
    half = rank // 2
    out_ref[...] = jnp.zeros_like(out_ref)
    max_ref[...] = jnp.zeros_like(max_ref)

    def group(first, count, coef):
        mats = coup_ref[pl.ds(first, count)].reshape(count * rank, rank)
        res = product_of(mats, coef)
        for q in range(count):
            row = pos_ref[first + q]
            one = res[q * rank : (q + 1) * rank]
            folded = jnp.concatenate([one[:half], one[half:]], axis=1)
            out_ref[row] = folded
            max_ref[pl.ds(row, 1), :] = jnp.max(jnp.abs(folded), axis=0, keepdims=True)

    def leaf_step(m, carry):
        group(m * K0, K0, leaf_ref[m])
        return carry

    def upper_step(m, carry):
        group(leaf_count * K0 + m * K1, K1, upper_ref[m])
        return carry

    lax.fori_loop(0, leaf_count, leaf_step, 0, unroll=4)
    lax.fori_loop(0, upper_count, upper_step, 0, unroll=2)


def halo_kernel(width_x, width_y, vec_ref, edge_ref, rows_ref, cols_ref, send_sem, recv_sem):
    here_x = lax.axis_index("qx")
    here_y = lax.axis_index("qy")
    rows = vec_ref.shape[1]
    leaf_x = edge_ref.shape[1]
    steps = [(1, 0), (-1, 0), (0, 1), (0, -1), (1, 1), (1, -1), (-1, 1), (-1, -1)]

    def present(dx, dy):
        x = here_x + dx
        y = here_y + dy
        return (x >= 0) & (x < width_x) & (y >= 0) & (y < width_y)

    def copy_of(n):
        dx, dy = steps[n]
        if dy == 0:
            first = rows - LS if dx > 0 else 0
            src = vec_ref.at[:, pl.ds(first, LS), :]
            dst = rows_ref.at[0 if dx > 0 else 1]
        else:
            side = 1 if dy > 0 else 0
            if dx == 0:
                src = edge_ref.at[side]
                dst = cols_ref.at[1 - side, pl.ds(1, leaf_x)]
            else:
                src = edge_ref.at[side, leaf_x - 1 if dx > 0 else 0]
                dst = cols_ref.at[1 - side, 0 if dx > 0 else leaf_x + 1]
        return pltpu.make_async_remote_copy(
            src_ref=src,
            dst_ref=dst,
            send_sem=send_sem.at[n],
            recv_sem=recv_sem.at[n],
            device_id=(here_x + dx, here_y + dy),
            device_id_type=pl.DeviceIdType.MESH,
        )

    barrier = pltpu.get_barrier_semaphore()
    for dx, dy in steps:

        @pl.when(present(dx, dy))
        def _():
            pl.semaphore_signal(
                barrier,
                inc=1,
                device_id=(here_x + dx, here_y + dy),
                device_id_type=pl.DeviceIdType.MESH,
            )

    spans = []
    for here, width in ((here_x, width_x), (here_y, width_y)):
        spans.append(1 + (here > 0).astype(jnp.int32) + (here < width - 1).astype(jnp.int32))
    pl.semaphore_wait(barrier, spans[0] * spans[1] - 1)

    for n, (dx, dy) in enumerate(steps):

        @pl.when(present(dx, dy))
        def _():
            copy_of(n).start()

    for n, (dx, dy) in enumerate(steps):

        @pl.when(present(dx, dy))
        def _():
            copy_of(n).wait_send()

        @pl.when(present(-dx, -dy))
        def _():
            copy_of(n).wait_recv()


def near_kernel(leaf_y, off_ref, tiles_ref, grid_ref, out_ref):
    vecs = grid_ref.shape[2]
    per = tiles_ref.shape[0]
    for u in range(per):
        m = pl.program_id(0) * per + u
        i = m // leaf_y
        j = lax.rem(m, leaf_y)
        total = None
        for k in range(tiles_ref.shape[1]):
            o = off_ref[m, k]
            x = (i + o // 3) * LS
            y = pl.multiple_of((j + lax.rem(o, 3)) * LS, LS)
            block = grid_ref[pl.ds(x, LS), pl.ds(y, LS), :].reshape(LS * LS, vecs)
            term = jnp.dot(tiles_ref[u, k], block, preferred_element_type=jnp.float32)
            total = term if total is None else total + term
        out_ref[u] = total


def far_kernel(leaf_x, leaf_y, tgt_ref, recv_ref, down_ref, row_ref, near_ref, out_ref, acc, full):
    leaf_count = leaf_x * leaf_y
    half = acc.shape[2] // 2
    acc[...] = jnp.zeros_like(acc)

    def add(r, carry):
        t = tgt_ref[r]
        acc[t] = acc[t] + recv_ref[r]
        return carry

    lax.fori_loop(0, recv_ref.shape[0], add, 0, unroll=4)

    def unfolded(n):
        value = acc[n]
        return jnp.concatenate([value[:, :half], value[:, half:]], axis=0)

    def leaf(m, carry):
        j = lax.rem(m, leaf_y)
        coef = unfolded(m) + product_of(down_ref[m], unfolded(leaf_count + j // 2))
        high, low = halves(coef)
        basis = row_ref[m]
        far = lax.dot_general(
            jnp.concatenate([basis, basis], axis=0),
            jnp.concatenate([high, low], axis=0),
            (((0,), (0,)), ((), ())),
            preferred_element_type=jnp.float32,
        )
        full[m] = near_ref[m] + far
        return carry

    lax.fori_loop(0, leaf_count, leaf, 0, unroll=4)
    for a in range(leaf_x):
        for i in range(LS):
            rows = [full[a * leaf_y + h, i * LS : (i + 1) * LS, :] for h in range(leaf_y)]
            out_ref[:, a * LS + i, :] = jnp.concatenate(rows, axis=0).T


def body(
    vectors,
    near_tiles,
    near_offset,
    col_basis,
    row_basis,
    up_transfer,
    down_transfer,
    coupling,
    couple_dest,
    couple_target,
):
    precise = lax.Precision.HIGHEST
    f32 = jnp.float32
    shape = jax.ShapeDtypeStruct
    width_x = lax.axis_size("qx")
    width_y = lax.axis_size("qy")
    devices = width_x * width_y
    vec_count, rows_x, rows_y = vectors.shape
    leaf_x = rows_x // LS
    leaf_y = rows_y // LS
    leaf_count = leaf_x * leaf_y
    upper_count = leaf_y // 2
    cluster_count = leaf_count + upper_count
    rank_size = coupling.shape[2]
    slot_count = coupling.shape[1]
    capacity = (slot_count + devices - 1) // devices
    near_count = near_tiles.shape[2]
    points = LS * LS
    fold = (rank_size // 2, 2 * vec_count)
    my_index = lax.axis_index("qx") * width_y + lax.axis_index("qy")

    minor = vectors.transpose(1, 2, 0)
    strips = jnp.stack([minor[:, :LS], minor[:, rows_y - LS :]]).reshape(2, leaf_x, LS, LS, vec_count)
    strips = jnp.concatenate([strips[:, :, : LS // 2], strips[:, :, LS // 2 :]], axis=-1)

    blocks = (
        vectors.reshape(vec_count, leaf_x, LS, leaf_y, LS)
        .transpose(1, 3, 0, 2, 4)
        .reshape(leaf_x, leaf_y, vec_count, points)
    )
    leaf_coef = jnp.einsum("ijrp,ijvp->ijrv", col_basis, blocks, preferred_element_type=f32)
    lifted = jnp.einsum("ijrs,ijsv->ijrv", up_transfer, leaf_coef, precision=precise)
    upper_coef = lifted.reshape(leaf_x, upper_count, 2, rank_size, vec_count).sum(axis=(0, 2))

    own_dest = lax.dynamic_index_in_dim(couple_dest, my_index, 0, keepdims=False)
    slot_ident = jnp.arange(slot_count, dtype=jnp.int32)
    same_dest = own_dest[:, None] == own_dest[None, :]
    earlier = slot_ident[:, None] > slot_ident[None, :]
    order_in = jnp.sum((same_dest & earlier).astype(jnp.int32), axis=1)
    spare_row = devices * capacity
    position = jnp.where(own_dest >= 0, own_dest * capacity + order_in, spare_row)
    placed, peaks = pl.pallas_call(
        lambda *refs: contrib_kernel(leaf_count, upper_count, *refs),
        out_shape=(shape((spare_row + 1,) + fold, f32), shape((spare_row + 1, fold[1]), f32)),
        in_specs=[SM, VM, VM, VM],
        out_specs=(VM, VM),
        cost_estimate=pl.CostEstimate(
            flops=8 * slot_count * rank_size * rank_size * vec_count,
            bytes_accessed=16 * slot_count * rank_size * rank_size * 4,
            transcendentals=0,
        ),
        name="contrib",
    )(position, coupling[0], leaf_coef.reshape(leaf_count, rank_size, vec_count), upper_coef)

    peak = jnp.max(peaks[:spare_row], axis=1)
    power = jnp.ceil(jnp.log2(jnp.maximum(peak, 1e-30)))
    scaled = placed[:spare_row] * jnp.exp2(TOP - power)[:, None, None]
    notes = jnp.broadcast_to(power.reshape(devices, capacity, 1), (devices, capacity, fold[1]))
    outgoing = jnp.concatenate(
        [
            scaled.reshape(devices, capacity * fold[0], fold[1]).astype(jnp.float16),
            notes.astype(jnp.float16),
        ],
        axis=1,
    )
    outgoing, strips = lax.optimization_barrier((outgoing, strips))
    arrived = lax.all_to_all(outgoing, ("qx", "qy"), split_axis=0, concat_axis=0, tiled=True)

    kind = vectors.dtype
    near_rows, near_cols = pl.pallas_call(
        lambda *refs: halo_kernel(width_x, width_y, *refs),
        out_shape=(
            shape((2, vec_count, LS, rows_y), kind),
            shape((2, leaf_x + 2, LS // 2, LS, 2 * vec_count), kind),
        ),
        in_specs=[ANY, ANY],
        out_specs=(ANY, ANY),
        scratch_shapes=[pltpu.SemaphoreType.DMA((8,)), pltpu.SemaphoreType.DMA((8,))],
        compiler_params=pltpu.CompilerParams(collective_id=0, has_side_effects=True),
        cost_estimate=pl.CostEstimate(
            flops=0, bytes_accessed=64 * vec_count * LS * rows_y * 2, transcendentals=0
        ),
        name="halo",
    )(vectors, strips)
    here_x = lax.axis_index("qx")
    here_y = lax.axis_index("qy")
    has_x = jnp.stack([here_x > 0, here_x < width_x - 1])
    has_y = jnp.stack([here_y > 0, here_y < width_y - 1])
    near_rows = jnp.where(has_x[:, None, None, None], near_rows, 0).transpose(0, 2, 3, 1)
    tall = jnp.concatenate([near_rows[0], minor, near_rows[1]], axis=0)
    along = jnp.concatenate([has_x[:1], jnp.ones((leaf_x,), bool), has_x[1:]])
    valid = has_y[:, None] & along[None, :]
    near_cols = jnp.where(valid[:, :, None, None, None], near_cols, 0)
    near_cols = jnp.concatenate(
        [near_cols[..., :vec_count], near_cols[..., vec_count:]], axis=2
    ).reshape(2, rows_x + 2 * LS, LS, vec_count)
    grid = jnp.concatenate([near_cols[0], tall, near_cols[1]], axis=1)
    per = 4 if leaf_count % 4 == 0 else 1
    near = pl.pallas_call(
        lambda *refs: near_kernel(leaf_y, *refs),
        grid=(leaf_count // per,),
        out_shape=shape((leaf_count, points, vec_count), f32),
        in_specs=[
            SM,
            pl.BlockSpec((per, near_count, points, points), lambda m: (m, 0, 0, 0)),
            VM,
        ],
        out_specs=pl.BlockSpec((per, points, vec_count), lambda m: (m, 0, 0)),
        cost_estimate=pl.CostEstimate(
            flops=2 * leaf_count * near_count * points * points * vec_count,
            bytes_accessed=leaf_count * near_count * points * points * 2,
            transcendentals=0,
        ),
        name="near",
    )(
        near_offset.reshape(leaf_count, near_count),
        near_tiles.reshape(leaf_count, near_count, points, points),
        grid,
    )

    matches = couple_dest == my_index
    counts = matches.astype(jnp.int32)
    order = jnp.cumsum(counts, axis=-1) - counts
    landing = matches[:, None, :] & (order[:, None, :] == jnp.arange(capacity, dtype=jnp.int32)[None, :, None])
    target = cluster_count + jnp.sum(
        jnp.where(landing, couple_target[:, None, :] - cluster_count, 0), axis=-1
    )

    rows = capacity * fold[0]
    exponent = arrived[:, rows:, :1].astype(f32).reshape(spare_row, 1, 1)
    recv = arrived[:, :rows].astype(f32).reshape((spare_row,) + fold) * jnp.exp2(exponent - TOP)
    return pl.pallas_call(
        lambda *refs: far_kernel(leaf_x, leaf_y, *refs),
        out_shape=shape((vec_count, rows_x, rows_y), f32),
        in_specs=[SM, VM, VM, VM, VM],
        out_specs=VM,
        scratch_shapes=[
            pltpu.VMEM((cluster_count + 1,) + fold, f32),
            pltpu.VMEM((leaf_count, points, vec_count), f32),
        ],
        name="far",
    )(
        target.reshape(spare_row),
        recv,
        down_transfer.reshape(leaf_count, rank_size, rank_size),
        row_basis.reshape(leaf_count, rank_size, points),
        near,
    )


def solution(mesh):
    return jax.shard_map(
        body,
        mesh=mesh,
        in_specs=(
            P(None, "qx", "qy"),
            P("qx", "qy", None, None, None),
            P("qx", "qy", None),
            P("qx", "qy", None, None),
            P("qx", "qy", None, None),
            P("qx", "qy", None, None),
            P("qx", "qy", None, None),
            P(("qx", "qy"), None, None, None),
            P(),
            P(),
        ),
        out_specs=P(None, "qx", "qy"),
        check_vma=False,
    )
```

```python
import jax
import jax.numpy as jnp
from jax import lax
from jax.experimental import pallas as pl
from jax.experimental.pallas import tpu as pltpu
from jax.sharding import PartitionSpec as P

LS = 16
K0 = 6
K1 = 8


ANY = pl.BlockSpec(memory_space=pl.ANY)
VM = pl.BlockSpec(memory_space=pltpu.VMEM)
SM = pl.BlockSpec(memory_space=pltpu.SMEM)
TOP = 14


def halves(value):
    high = value.astype(jnp.bfloat16)
    return high, (value - high.astype(jnp.float32)).astype(jnp.bfloat16)


def product_of(left, right):
    lh, ll = halves(left)
    rh, rl = halves(right)
    return jnp.dot(
        jnp.concatenate([lh, ll, lh, ll], axis=1),
        jnp.concatenate([rh, rh, rl, rl], axis=0),
        preferred_element_type=jnp.float32,
    )


def contributions(leaf_count, upper_count, slot_ref, coup_ref, leaf_ref, upper_ref, out_ref, max_ref, held):
    rank = coup_ref.shape[1]
    half = rank // 2
    held[held.shape[0] - 1] = jnp.zeros_like(held[0])

    def group(first, count, coef):
        mats = coup_ref[pl.ds(first, count)].reshape(count * rank, rank)
        res = product_of(mats, coef)
        for q in range(count):
            one = res[q * rank : (q + 1) * rank]
            held[first + q] = jnp.concatenate([one[:half], one[half:]], axis=1)

    def leaf_step(m, carry):
        group(m * K0, K0, leaf_ref[m])
        return carry

    def upper_step(m, carry):
        group(leaf_count * K0 + m * K1, K1, upper_ref[m])
        return carry

    def place(p, carry):
        value = held[slot_ref[p]]
        out_ref[p] = value
        max_ref[pl.ds(p, 1), :] = jnp.max(jnp.abs(value), axis=0, keepdims=True)
        return carry

    lax.fori_loop(0, leaf_count, leaf_step, 0, unroll=4)
    lax.fori_loop(0, upper_count, upper_step, 0, unroll=2)
    lax.fori_loop(0, out_ref.shape[0], place, 0, unroll=4)


def first_kernel(
    leaf_count,
    upper_count,
    width_x,
    width_y,
    slot_ref,
    coup_ref,
    leaf_ref,
    upper_ref,
    vec_ref,
    edge_ref,
    out_ref,
    max_ref,
    rows_ref,
    cols_ref,
    held,
    send_sem,
    recv_sem,
):
    here_x = lax.axis_index("qx")
    here_y = lax.axis_index("qy")
    rows = vec_ref.shape[1]
    leaf_x = edge_ref.shape[1]
    steps = [(1, 0), (-1, 0), (0, 1), (0, -1), (1, 1), (1, -1), (-1, 1), (-1, -1)]

    def present(dx, dy):
        x = here_x + dx
        y = here_y + dy
        return (x >= 0) & (x < width_x) & (y >= 0) & (y < width_y)

    def copy_of(n):
        dx, dy = steps[n]
        if dy == 0:
            first = rows - LS if dx > 0 else 0
            src = vec_ref.at[:, pl.ds(first, LS), :]
            dst = rows_ref.at[0 if dx > 0 else 1]
        else:
            side = 1 if dy > 0 else 0
            if dx == 0:
                src = edge_ref.at[side]
                dst = cols_ref.at[1 - side, pl.ds(1, leaf_x)]
            else:
                src = edge_ref.at[side, leaf_x - 1 if dx > 0 else 0]
                dst = cols_ref.at[1 - side, 0 if dx > 0 else leaf_x + 1]
        return pltpu.make_async_remote_copy(
            src_ref=src,
            dst_ref=dst,
            send_sem=send_sem.at[n],
            recv_sem=recv_sem.at[n],
            device_id=(here_x + dx, here_y + dy),
            device_id_type=pl.DeviceIdType.MESH,
        )

    barrier = pltpu.get_barrier_semaphore()
    for dx, dy in steps:

        @pl.when(present(dx, dy))
        def _():
            pl.semaphore_signal(
                barrier,
                inc=1,
                device_id=(here_x + dx, here_y + dy),
                device_id_type=pl.DeviceIdType.MESH,
            )

    spans = []
    for here, width in ((here_x, width_x), (here_y, width_y)):
        spans.append(1 + (here > 0).astype(jnp.int32) + (here < width - 1).astype(jnp.int32))
    pl.semaphore_wait(barrier, spans[0] * spans[1] - 1)

    for n, (dx, dy) in enumerate(steps):

        @pl.when(present(dx, dy))
        def _():
            copy_of(n).start()

    contributions(
        leaf_count, upper_count, slot_ref, coup_ref, leaf_ref, upper_ref, out_ref, max_ref, held
    )

    for n, (dx, dy) in enumerate(steps):

        @pl.when(present(dx, dy))
        def _():
            copy_of(n).wait_send()

        @pl.when(present(-dx, -dy))
        def _():
            copy_of(n).wait_recv()


def near_kernel(leaf_y, off_ref, tiles_ref, grid_ref, out_ref):
    vecs = grid_ref.shape[2]
    per = tiles_ref.shape[0]
    for u in range(per):
        m = pl.program_id(0) * per + u
        i = m // leaf_y
        j = lax.rem(m, leaf_y)
        total = None
        for k in range(tiles_ref.shape[1]):
            o = off_ref[m, k]
            x = (i + o // 3) * LS
            y = pl.multiple_of((j + lax.rem(o, 3)) * LS, LS)
            block = grid_ref[pl.ds(x, LS), pl.ds(y, LS), :].reshape(LS * LS, vecs)
            term = jnp.dot(tiles_ref[u, k], block, preferred_element_type=jnp.float32)
            total = term if total is None else total + term
        out_ref[u] = total


def far_kernel(leaf_x, leaf_y, tgt_ref, recv_ref, down_ref, row_ref, near_ref, out_ref, acc, full):
    leaf_count = leaf_x * leaf_y
    half = acc.shape[2] // 2
    acc[...] = jnp.zeros_like(acc)

    def add(r, carry):
        t = tgt_ref[r]
        acc[t] = acc[t] + recv_ref[r]
        return carry

    lax.fori_loop(0, recv_ref.shape[0], add, 0, unroll=4)

    def unfolded(n):
        value = acc[n]
        return jnp.concatenate([value[:, :half], value[:, half:]], axis=0)

    def leaf(m, carry):
        j = lax.rem(m, leaf_y)
        coef = unfolded(m) + product_of(down_ref[m], unfolded(leaf_count + j // 2))
        high, low = halves(coef)
        basis = row_ref[m]
        far = lax.dot_general(
            jnp.concatenate([basis, basis], axis=0),
            jnp.concatenate([high, low], axis=0),
            (((0,), (0,)), ((), ())),
            preferred_element_type=jnp.float32,
        )
        full[m] = near_ref[m] + far
        return carry

    lax.fori_loop(0, leaf_count, leaf, 0, unroll=4)
    for a in range(leaf_x):
        for i in range(LS):
            rows = [full[a * leaf_y + h, i * LS : (i + 1) * LS, :] for h in range(leaf_y)]
            out_ref[:, a * LS + i, :] = jnp.concatenate(rows, axis=0).T


def body(
    vectors,
    near_tiles,
    near_offset,
    col_basis,
    row_basis,
    up_transfer,
    down_transfer,
    coupling,
    couple_dest,
    couple_target,
):
    precise = lax.Precision.HIGHEST
    f32 = jnp.float32
    shape = jax.ShapeDtypeStruct
    width_x = lax.axis_size("qx")
    width_y = lax.axis_size("qy")
    devices = width_x * width_y
    vec_count, rows_x, rows_y = vectors.shape
    leaf_x = rows_x // LS
    leaf_y = rows_y // LS
    leaf_count = leaf_x * leaf_y
    upper_count = leaf_y // 2
    cluster_count = leaf_count + upper_count
    rank_size = coupling.shape[2]
    slot_count = coupling.shape[1]
    capacity = (slot_count + devices - 1) // devices
    near_count = near_tiles.shape[2]
    points = LS * LS
    fold = (rank_size // 2, 2 * vec_count)
    my_index = lax.axis_index("qx") * width_y + lax.axis_index("qy")

    minor = vectors.transpose(1, 2, 0)
    strips = jnp.stack([minor[:, :LS], minor[:, rows_y - LS :]]).reshape(2, leaf_x, LS, LS, vec_count)
    strips = jnp.concatenate([strips[:, :, : LS // 2], strips[:, :, LS // 2 :]], axis=-1)

    blocks = (
        vectors.reshape(vec_count, leaf_x, LS, leaf_y, LS)
        .transpose(1, 3, 0, 2, 4)
        .reshape(leaf_x, leaf_y, vec_count, points)
    )
    leaf_coef = jnp.einsum("ijrp,ijvp->ijrv", col_basis, blocks, preferred_element_type=f32)
    lifted = jnp.einsum("ijrs,ijsv->ijrv", up_transfer, leaf_coef, precision=precise)
    upper_coef = lifted.reshape(leaf_x, upper_count, 2, rank_size, vec_count).sum(axis=(0, 2))

    own_dest = lax.dynamic_index_in_dim(couple_dest, my_index, 0, keepdims=False)
    slot_ident = jnp.arange(slot_count, dtype=jnp.int32)
    same_dest = own_dest[:, None] == own_dest[None, :]
    earlier = slot_ident[:, None] > slot_ident[None, :]
    order_in = jnp.sum((same_dest & earlier).astype(jnp.int32), axis=1)
    spare_row = devices * capacity
    position = jnp.where(own_dest >= 0, own_dest * capacity + order_in, spare_row)
    filled = position[None, :] == jnp.arange(spare_row, dtype=jnp.int32)[:, None]
    slot_of = slot_count + jnp.sum(jnp.where(filled, slot_ident - slot_count, 0), axis=1)
    kind = vectors.dtype
    placed, peaks, near_rows, near_cols = pl.pallas_call(
        lambda *refs: first_kernel(leaf_count, upper_count, width_x, width_y, *refs),
        out_shape=(
            shape((spare_row,) + fold, f32),
            shape((spare_row, fold[1]), f32),
            shape((2, vec_count, LS, rows_y), kind),
            shape((2, leaf_x + 2, LS // 2, LS, 2 * vec_count), kind),
        ),
        in_specs=[SM, VM, VM, VM, ANY, ANY],
        out_specs=(VM, VM, ANY, ANY),
        scratch_shapes=[
            pltpu.VMEM((slot_count + 1,) + fold, f32),
            pltpu.SemaphoreType.DMA((8,)),
            pltpu.SemaphoreType.DMA((8,)),
        ],
        compiler_params=pltpu.CompilerParams(collective_id=0, has_side_effects=True),
        name="contrib",
    )(
        slot_of,
        coupling[0],
        leaf_coef.reshape(leaf_count, rank_size, vec_count),
        upper_coef,
        vectors,
        strips,
    )

    peak = jnp.max(peaks, axis=1)
    power = jnp.ceil(jnp.log2(jnp.maximum(peak, 1e-30)))
    scaled = placed * jnp.exp2(TOP - power)[:, None, None]
    notes = jnp.broadcast_to(power.reshape(devices, capacity, 1), (devices, capacity, fold[1]))
    outgoing = jnp.concatenate(
        [
            scaled.reshape(devices, capacity * fold[0], fold[1]).astype(jnp.float16),
            notes.astype(jnp.float16),
        ],
        axis=1,
    )
    outgoing, near_rows, near_cols = lax.optimization_barrier((outgoing, near_rows, near_cols))
    arrived = lax.all_to_all(outgoing, ("qx", "qy"), split_axis=0, concat_axis=0, tiled=True)

    here_x = lax.axis_index("qx")
    here_y = lax.axis_index("qy")
    has_x = jnp.stack([here_x > 0, here_x < width_x - 1])
    has_y = jnp.stack([here_y > 0, here_y < width_y - 1])
    near_rows = jnp.where(has_x[:, None, None, None], near_rows, 0).transpose(0, 2, 3, 1)
    tall = jnp.concatenate([near_rows[0], minor, near_rows[1]], axis=0)
    along = jnp.concatenate([has_x[:1], jnp.ones((leaf_x,), bool), has_x[1:]])
    valid = has_y[:, None] & along[None, :]
    near_cols = jnp.where(valid[:, :, None, None, None], near_cols, 0)
    near_cols = jnp.concatenate(
        [near_cols[..., :vec_count], near_cols[..., vec_count:]], axis=2
    ).reshape(2, rows_x + 2 * LS, LS, vec_count)
    grid = jnp.concatenate([near_cols[0], tall, near_cols[1]], axis=1)
    per = 4 if leaf_count % 4 == 0 else 1
    near = pl.pallas_call(
        lambda *refs: near_kernel(leaf_y, *refs),
        grid=(leaf_count // per,),
        out_shape=shape((leaf_count, points, vec_count), f32),
        in_specs=[
            SM,
            pl.BlockSpec((per, near_count, points, points), lambda m: (m, 0, 0, 0)),
            VM,
        ],
        out_specs=pl.BlockSpec((per, points, vec_count), lambda m: (m, 0, 0)),
        cost_estimate=pl.CostEstimate(
            flops=2 * leaf_count * near_count * points * points * vec_count,
            bytes_accessed=leaf_count * near_count * points * points * 2,
            transcendentals=0,
        ),
        name="near",
    )(
        near_offset.reshape(leaf_count, near_count),
        near_tiles.reshape(leaf_count, near_count, points, points),
        grid,
    )

    matches = couple_dest == my_index
    counts = matches.astype(jnp.int32)
    order = jnp.cumsum(counts, axis=-1) - counts
    landing = matches[:, None, :] & (order[:, None, :] == jnp.arange(capacity, dtype=jnp.int32)[None, :, None])
    target = cluster_count + jnp.sum(
        jnp.where(landing, couple_target[:, None, :] - cluster_count, 0), axis=-1
    )

    rows = capacity * fold[0]
    exponent = arrived[:, rows:, :1].astype(f32).reshape(spare_row, 1, 1)
    recv = arrived[:, :rows].astype(f32).reshape((spare_row,) + fold) * jnp.exp2(exponent - TOP)
    return pl.pallas_call(
        lambda *refs: far_kernel(leaf_x, leaf_y, *refs),
        out_shape=shape((vec_count, rows_x, rows_y), f32),
        in_specs=[SM, VM, VM, VM, VM],
        out_specs=VM,
        scratch_shapes=[
            pltpu.VMEM((cluster_count + 1,) + fold, f32),
            pltpu.VMEM((leaf_count, points, vec_count), f32),
        ],
        name="far",
    )(
        target.reshape(spare_row),
        recv,
        down_transfer.reshape(leaf_count, rank_size, rank_size),
        row_basis.reshape(leaf_count, rank_size, points),
        near,
    )


def solution(mesh):
    return jax.shard_map(
        body,
        mesh=mesh,
        in_specs=(
            P(None, "qx", "qy"),
            P("qx", "qy", None, None, None),
            P("qx", "qy", None),
            P("qx", "qy", None, None),
            P("qx", "qy", None, None),
            P("qx", "qy", None, None),
            P("qx", "qy", None, None),
            P(("qx", "qy"), None, None, None),
            P(),
            P(),
        ),
        out_specs=P(None, "qx", "qy"),
        check_vma=False,
    )
```

```python
import jax
import jax.numpy as jnp
from jax import lax
from jax.experimental import pallas as pl
from jax.experimental.pallas import tpu as pltpu
from jax.sharding import PartitionSpec as P

LS = 16
K0 = 6
K1 = 8


ANY = pl.BlockSpec(memory_space=pl.ANY)
VM = pl.BlockSpec(memory_space=pltpu.VMEM)
SM = pl.BlockSpec(memory_space=pltpu.SMEM)
TOP = 14


def halves(value):
    high = value.astype(jnp.bfloat16)
    return high, (value - high.astype(jnp.float32)).astype(jnp.bfloat16)


def product_of(left, right):
    lh, ll = halves(left)
    rh, rl = halves(right)
    return jnp.dot(
        jnp.concatenate([lh, ll, lh, ll], axis=1),
        jnp.concatenate([rh, rh, rl, rl], axis=0),
        preferred_element_type=jnp.float32,
    )


def contributions(leaf_count, upper_count, slot_ref, coup_ref, leaf_ref, upper_ref, out_ref, max_ref, mats_ref, held):
    rank = coup_ref.shape[1]
    half = rank // 2
    held[held.shape[0] - 1] = jnp.zeros_like(held[0])

    def group(first, count, coef):
        mats = mats_ref[pl.ds(first, count)].reshape(count * rank, rank)
        res = product_of(mats, coef)
        for q in range(count):
            one = res[q * rank : (q + 1) * rank]
            held[first + q] = jnp.concatenate([one[:half], one[half:]], axis=1)

    def leaf_step(m, carry):
        group(m * K0, K0, leaf_ref[m])
        return carry

    def upper_step(m, carry):
        group(leaf_count * K0 + m * K1, K1, upper_ref[m])
        return carry

    def place(p, carry):
        value = held[slot_ref[p]]
        out_ref[p] = value
        max_ref[pl.ds(p, 1), :] = jnp.max(jnp.abs(value), axis=0, keepdims=True)
        return carry

    def turn(r, carry):
        mats_ref[:, r, :] = coup_ref[r].T
        return carry

    lax.fori_loop(0, rank, turn, 0, unroll=4)
    lax.fori_loop(0, leaf_count, leaf_step, 0, unroll=4)
    lax.fori_loop(0, upper_count, upper_step, 0, unroll=2)
    lax.fori_loop(0, out_ref.shape[0], place, 0, unroll=4)


def first_kernel(
    leaf_count,
    upper_count,
    width_x,
    width_y,
    slot_ref,
    coup_ref,
    leaf_ref,
    upper_ref,
    vec_ref,
    edge_ref,
    out_ref,
    max_ref,
    rows_ref,
    cols_ref,
    mats_ref,
    held,
    send_sem,
    recv_sem,
):
    here_x = lax.axis_index("qx")
    here_y = lax.axis_index("qy")
    rows = vec_ref.shape[1]
    leaf_x = edge_ref.shape[1]
    steps = [(1, 0), (-1, 0), (0, 1), (0, -1), (1, 1), (1, -1), (-1, 1), (-1, -1)]

    def present(dx, dy):
        x = here_x + dx
        y = here_y + dy
        return (x >= 0) & (x < width_x) & (y >= 0) & (y < width_y)

    def copy_of(n):
        dx, dy = steps[n]
        if dy == 0:
            first = rows - LS if dx > 0 else 0
            src = vec_ref.at[:, pl.ds(first, LS), :]
            dst = rows_ref.at[0 if dx > 0 else 1]
        else:
            side = 1 if dy > 0 else 0
            if dx == 0:
                src = edge_ref.at[side]
                dst = cols_ref.at[1 - side, pl.ds(1, leaf_x)]
            else:
                src = edge_ref.at[side, leaf_x - 1 if dx > 0 else 0]
                dst = cols_ref.at[1 - side, 0 if dx > 0 else leaf_x + 1]
        return pltpu.make_async_remote_copy(
            src_ref=src,
            dst_ref=dst,
            send_sem=send_sem.at[n],
            recv_sem=recv_sem.at[n],
            device_id=(here_x + dx, here_y + dy),
            device_id_type=pl.DeviceIdType.MESH,
        )

    barrier = pltpu.get_barrier_semaphore()
    for dx, dy in steps:

        @pl.when(present(dx, dy))
        def _():
            pl.semaphore_signal(
                barrier,
                inc=1,
                device_id=(here_x + dx, here_y + dy),
                device_id_type=pl.DeviceIdType.MESH,
            )

    spans = []
    for here, width in ((here_x, width_x), (here_y, width_y)):
        spans.append(1 + (here > 0).astype(jnp.int32) + (here < width - 1).astype(jnp.int32))
    pl.semaphore_wait(barrier, spans[0] * spans[1] - 1)

    for n, (dx, dy) in enumerate(steps):

        @pl.when(present(dx, dy))
        def _():
            copy_of(n).start()

    contributions(
        leaf_count, upper_count, slot_ref, coup_ref, leaf_ref, upper_ref, out_ref, max_ref, mats_ref, held
    )

    for n, (dx, dy) in enumerate(steps):

        @pl.when(present(dx, dy))
        def _():
            copy_of(n).wait_send()

        @pl.when(present(-dx, -dy))
        def _():
            copy_of(n).wait_recv()


def near_kernel(leaf_y, off_ref, tiles_ref, grid_ref, out_ref):
    vecs = grid_ref.shape[2]
    per = tiles_ref.shape[0]
    for u in range(per):
        m = pl.program_id(0) * per + u
        i = m // leaf_y
        j = lax.rem(m, leaf_y)
        total = None
        for k in range(tiles_ref.shape[1]):
            o = off_ref[m, k]
            x = (i + o // 3) * LS
            y = pl.multiple_of((j + lax.rem(o, 3)) * LS, LS)
            block = grid_ref[pl.ds(x, LS), pl.ds(y, LS), :].reshape(LS * LS, vecs)
            term = jnp.dot(tiles_ref[u, k], block, preferred_element_type=jnp.float32)
            total = term if total is None else total + term
        out_ref[u] = total


def far_kernel(leaf_x, leaf_y, tgt_ref, recv_ref, down_ref, row_ref, near_ref, out_ref, acc, full):
    leaf_count = leaf_x * leaf_y
    half = acc.shape[2] // 2
    acc[...] = jnp.zeros_like(acc)

    def add(r, carry):
        t = tgt_ref[r]
        acc[t] = acc[t] + recv_ref[r]
        return carry

    lax.fori_loop(0, recv_ref.shape[0], add, 0, unroll=4)

    def unfolded(n):
        value = acc[n]
        return jnp.concatenate([value[:, :half], value[:, half:]], axis=0)

    def leaf(m, carry):
        j = lax.rem(m, leaf_y)
        coef = unfolded(m) + product_of(down_ref[m], unfolded(leaf_count + j // 2))
        high, low = halves(coef)
        basis = row_ref[m]
        far = lax.dot_general(
            jnp.concatenate([basis, basis], axis=0),
            jnp.concatenate([high, low], axis=0),
            (((0,), (0,)), ((), ())),
            preferred_element_type=jnp.float32,
        )
        full[m] = near_ref[m] + far
        return carry

    lax.fori_loop(0, leaf_count, leaf, 0, unroll=4)
    for a in range(leaf_x):
        for i in range(LS):
            rows = [full[a * leaf_y + h, i * LS : (i + 1) * LS, :] for h in range(leaf_y)]
            out_ref[:, a * LS + i, :] = jnp.concatenate(rows, axis=0).T


def body(
    vectors,
    near_tiles,
    near_offset,
    col_basis,
    row_basis,
    up_transfer,
    down_transfer,
    coupling,
    couple_dest,
    couple_target,
):
    precise = lax.Precision.HIGHEST
    f32 = jnp.float32
    shape = jax.ShapeDtypeStruct
    width_x = lax.axis_size("qx")
    width_y = lax.axis_size("qy")
    devices = width_x * width_y
    vec_count, rows_x, rows_y = vectors.shape
    leaf_x = rows_x // LS
    leaf_y = rows_y // LS
    leaf_count = leaf_x * leaf_y
    upper_count = leaf_y // 2
    cluster_count = leaf_count + upper_count
    rank_size = coupling.shape[2]
    slot_count = coupling.shape[1]
    capacity = (slot_count + devices - 1) // devices
    near_count = near_tiles.shape[2]
    points = LS * LS
    fold = (rank_size // 2, 2 * vec_count)
    my_index = lax.axis_index("qx") * width_y + lax.axis_index("qy")

    minor = vectors.transpose(1, 2, 0)
    strips = jnp.stack([minor[:, :LS], minor[:, rows_y - LS :]]).reshape(2, leaf_x, LS, LS, vec_count)
    strips = jnp.concatenate([strips[:, :, : LS // 2], strips[:, :, LS // 2 :]], axis=-1)

    blocks = (
        vectors.reshape(vec_count, leaf_x, LS, leaf_y, LS)
        .transpose(1, 3, 0, 2, 4)
        .reshape(leaf_x, leaf_y, vec_count, points)
    )
    leaf_coef = jnp.einsum("ijrp,ijvp->ijrv", col_basis, blocks, preferred_element_type=f32)
    lifted = jnp.einsum("ijrs,ijsv->ijrv", up_transfer, leaf_coef, precision=precise)
    upper_coef = lifted.reshape(leaf_x, upper_count, 2, rank_size, vec_count).sum(axis=(0, 2))

    own_dest = lax.dynamic_index_in_dim(couple_dest, my_index, 0, keepdims=False)
    slot_ident = jnp.arange(slot_count, dtype=jnp.int32)
    same_dest = own_dest[:, None] == own_dest[None, :]
    earlier = slot_ident[:, None] > slot_ident[None, :]
    order_in = jnp.sum((same_dest & earlier).astype(jnp.int32), axis=1)
    spare_row = devices * capacity
    position = jnp.where(own_dest >= 0, own_dest * capacity + order_in, spare_row)
    filled = position[None, :] == jnp.arange(spare_row, dtype=jnp.int32)[:, None]
    slot_of = slot_count + jnp.sum(jnp.where(filled, slot_ident - slot_count, 0), axis=1)
    kind = vectors.dtype
    placed, peaks, near_rows, near_cols = pl.pallas_call(
        lambda *refs: first_kernel(leaf_count, upper_count, width_x, width_y, *refs),
        out_shape=(
            shape((spare_row,) + fold, f32),
            shape((spare_row, fold[1]), f32),
            shape((2, vec_count, LS, rows_y), kind),
            shape((2, leaf_x + 2, LS // 2, LS, 2 * vec_count), kind),
        ),
        in_specs=[SM, VM, VM, VM, ANY, ANY],
        out_specs=(VM, VM, ANY, ANY),
        scratch_shapes=[
            pltpu.VMEM((slot_count, rank_size, rank_size), f32),
            pltpu.VMEM((slot_count + 1,) + fold, f32),
            pltpu.SemaphoreType.DMA((8,)),
            pltpu.SemaphoreType.DMA((8,)),
        ],
        compiler_params=pltpu.CompilerParams(collective_id=0, has_side_effects=True),
        name="contrib",
    )(
        slot_of,
        coupling[0].transpose(1, 2, 0),
        leaf_coef.reshape(leaf_count, rank_size, vec_count),
        upper_coef,
        vectors,
        strips,
    )

    peak = jnp.max(peaks, axis=1)
    power = jnp.ceil(jnp.log2(jnp.maximum(peak, 1e-30)))
    scaled = placed * jnp.exp2(TOP - power)[:, None, None]
    notes = jnp.broadcast_to(power.reshape(devices, capacity, 1), (devices, capacity, fold[1]))
    outgoing = jnp.concatenate(
        [
            scaled.reshape(devices, capacity * fold[0], fold[1]).astype(jnp.float16),
            notes.astype(jnp.float16),
        ],
        axis=1,
    )
    outgoing, near_rows, near_cols = lax.optimization_barrier((outgoing, near_rows, near_cols))
    arrived = lax.all_to_all(outgoing, ("qx", "qy"), split_axis=0, concat_axis=0, tiled=True)

    here_x = lax.axis_index("qx")
    here_y = lax.axis_index("qy")
    has_x = jnp.stack([here_x > 0, here_x < width_x - 1])
    has_y = jnp.stack([here_y > 0, here_y < width_y - 1])
    near_rows = jnp.where(has_x[:, None, None, None], near_rows, 0).transpose(0, 2, 3, 1)
    tall = jnp.concatenate([near_rows[0], minor, near_rows[1]], axis=0)
    along = jnp.concatenate([has_x[:1], jnp.ones((leaf_x,), bool), has_x[1:]])
    valid = has_y[:, None] & along[None, :]
    near_cols = jnp.where(valid[:, :, None, None, None], near_cols, 0)
    near_cols = jnp.concatenate(
        [near_cols[..., :vec_count], near_cols[..., vec_count:]], axis=2
    ).reshape(2, rows_x + 2 * LS, LS, vec_count)
    grid = jnp.concatenate([near_cols[0], tall, near_cols[1]], axis=1)
    per = 4 if leaf_count % 4 == 0 else 1
    near = pl.pallas_call(
        lambda *refs: near_kernel(leaf_y, *refs),
        grid=(leaf_count // per,),
        out_shape=shape((leaf_count, points, vec_count), f32),
        in_specs=[
            SM,
            pl.BlockSpec((per, near_count, points, points), lambda m: (m, 0, 0, 0)),
            VM,
        ],
        out_specs=pl.BlockSpec((per, points, vec_count), lambda m: (m, 0, 0)),
        cost_estimate=pl.CostEstimate(
            flops=2 * leaf_count * near_count * points * points * vec_count,
            bytes_accessed=leaf_count * near_count * points * points * 2,
            transcendentals=0,
        ),
        name="near",
    )(
        near_offset.reshape(leaf_count, near_count),
        near_tiles.reshape(leaf_count, near_count, points, points),
        grid,
    )

    matches = couple_dest == my_index
    counts = matches.astype(jnp.int32)
    order = jnp.cumsum(counts, axis=-1) - counts
    landing = matches[:, None, :] & (order[:, None, :] == jnp.arange(capacity, dtype=jnp.int32)[None, :, None])
    target = cluster_count + jnp.sum(
        jnp.where(landing, couple_target[:, None, :] - cluster_count, 0), axis=-1
    )

    rows = capacity * fold[0]
    exponent = arrived[:, rows:, :1].astype(f32).reshape(spare_row, 1, 1)
    recv = arrived[:, :rows].astype(f32).reshape((spare_row,) + fold) * jnp.exp2(exponent - TOP)
    return pl.pallas_call(
        lambda *refs: far_kernel(leaf_x, leaf_y, *refs),
        out_shape=shape((vec_count, rows_x, rows_y), f32),
        in_specs=[SM, VM, VM, VM, VM],
        out_specs=VM,
        scratch_shapes=[
            pltpu.VMEM((cluster_count + 1,) + fold, f32),
            pltpu.VMEM((leaf_count, points, vec_count), f32),
        ],
        name="far",
    )(
        target.reshape(spare_row),
        recv,
        down_transfer.reshape(leaf_count, rank_size, rank_size),
        row_basis.reshape(leaf_count, rank_size, points),
        near,
    )


def solution(mesh):
    return jax.shard_map(
        body,
        mesh=mesh,
        in_specs=(
            P(None, "qx", "qy"),
            P("qx", "qy", None, None, None),
            P("qx", "qy", None),
            P("qx", "qy", None, None),
            P("qx", "qy", None, None),
            P("qx", "qy", None, None),
            P("qx", "qy", None, None),
            P(("qx", "qy"), None, None, None),
            P(),
            P(),
        ),
        out_specs=P(None, "qx", "qy"),
        check_vma=False,
    )
```
